32 devices in a mesh: ax: 8 (over z, x), sec: 4 (over y, core).
Axes of the slice: x: 2, y: 2, z: 4, core: 2. Of those that a mesh axis runs over, the one named last changes fastest.
Arguments:
- density: float32 [16, 256, 512], P('ax', None, 'sec'), may hold values from 0.7 to 1.4
- velocity: float32 [3, 16, 256, 512], P(None, 'ax', None, 'sec'), may hold values from -2.5 to 2.5
- pressure: float32 [16, 256, 512], P('ax', None, 'sec'), may hold values from 0.6 to 1.6
- cutoff: int32 [64], replicated, may hold values from 2 to 129, as said below
Outputs:
- density_new: float32 [16, 256, 512], P('ax', None, 'sec')
- velocity_new: float32 [3, 16, 256, 512], P(None, 'ax', None, 'sec')
- pressure_new: float32 [16, 256, 512], P('ax', None, 'sec')
The draws below stay inside these ranges and needn't reach their ends.
Inputs may be any that keep to these rules, and one draw needn't show every extreme that they name: cutoff[j] is the number of azimuthal modes kept in cycle j.
All inputs are finite; a program needn't handle non-finite values.
Results may differ from the reference program's by a relative error of at most 0.00005.
Values sent between devices are 32-bit elements; how exact they have to be, the bound alone decides.
A program may use at most 64 MiB of HBM per device.

```python
import math
import jax
import jax.numpy as jnp

NR = 256
NT = 512
NF = 64
NX = 16


def draw_cutoff(key, part):
    cycle_index = jnp.arange(NF, dtype=jnp.int32)
    extra_modes = jax.random.randint(key, (NF,), 0, 3, dtype=jnp.int32)
    counted = jnp.minimum(2 * cycle_index + 2 + extra_modes, 2 * NF + 1)
    return jnp.where(cycle_index == NF - 1, 2 * NF + 1, counted).astype(jnp.int32)


def block_scale(key, shape, pieces, smallest, largest):
    factor_of = 1.0
    for position, blocks in pieces:
        draws = jax.random.uniform(jax.random.fold_in(jax.random.fold_in(key, 6), position), (blocks,), jnp.float32, smallest / len(pieces), largest / len(pieces))
        factor_of = factor_of * jnp.repeat(jnp.exp(draws), shape[position] // blocks).reshape((-1,) + (1,) * (len(shape) - 1 - position))
    return factor_of


def gaussian(key, extent, spread, most, shards=(), held_as=jnp.bfloat16):
    values = spread * jax.random.normal(key, extent, jnp.float32)
    if shards:
        values = values * block_scale(key, extent, shards, -0.22, 0.18)
    return jnp.clip(values, -most, most).astype(held_as)


def setup_inputs(seed: int = 0) -> dict:
    keys = jax.random.split(jax.random.key(seed), 5)
    return {
        "density": jnp.clip(jnp.exp(math.log(1.4) - 0.6931472 * jax.random.uniform(keys[0], (NX, NR, NT), jnp.float32) ** block_scale(keys[0], (NX, NR, NT), ((0, 8), (2, 4)), -0.2, 0.2)), 0.7, 1.4),
        "velocity": gaussian(keys[1], (3, NX, NR, NT), 0.25, 2.5, ((1, 8), (3, 4)), jnp.float32),
        "pressure": jnp.clip(jnp.exp(math.log(1.6) - 0.98082923 * jax.random.uniform(keys[2], (NX, NR, NT), jnp.float32) ** block_scale(keys[2], (NX, NR, NT), ((0, 8), (2, 4)), -0.2, 0.2)), 0.6, 1.6),
        "cutoff": draw_cutoff(jax.random.fold_in(keys[4], 71), 0),
    }


def tendency(state, x_plus, x_minus, r_plus, r_minus, t_plus, t_minus, spacing, angle_step):
    radial_cells = state.shape[2]
    inv_r = 1.0 / ((jnp.arange(radial_cells, dtype=jnp.float32) + 0.5) * spacing)
    inv_r = inv_r[:, None]
    grad_x = (x_plus - x_minus) * (0.5 / spacing)
    grad_r = (r_plus - r_minus) * (0.5 / spacing)
    grad_t = (t_plus - t_minus) * (0.5 / angle_step) * inv_r
    density_now = state[0]
    axial = state[1]
    radial = state[2]
    azimuthal = state[3]
    pressure_now = state[4]
    advect = axial * grad_x + radial * grad_r + azimuthal * grad_t
    diverg = grad_x[1] + grad_r[2] + radial * inv_r + grad_t[3]
    rate_density = -advect[0] - density_now * diverg
    rate_axial = -advect[1] - grad_x[4] / density_now
    rate_radial = -advect[2] + azimuthal * azimuthal * inv_r - grad_r[4] / density_now
    rate_azimuthal = -advect[3] - radial * azimuthal * inv_r - grad_t[4] / density_now
    rate_pressure = -advect[4] - 1.4 * pressure_now * diverg
    return jnp.stack([rate_density, rate_axial, rate_radial, rate_azimuthal, rate_pressure], axis=0)


def neighbours(state):
    axis_sign = jnp.array([1.0, 1.0, -1.0, -1.0, 1.0], dtype=jnp.float32)[:, None, None]
    wall_sign = jnp.array([1.0, 1.0, -1.0, 1.0, 1.0], dtype=jnp.float32)[:, None, None]
    x_plus = jnp.roll(state, -1, axis=1)
    x_minus = jnp.roll(state, 1, axis=1)
    t_plus = jnp.roll(state, -1, axis=3)
    t_minus = jnp.roll(state, 1, axis=3)
    across = jnp.roll(state[:, :, 0, :], NT // 2, axis=-1) * axis_sign
    wall_rows = state[:, :, -1, :] * wall_sign
    r_minus = jnp.concatenate([across[:, :, None], state[:, :, :-1]], axis=2)
    r_plus = jnp.concatenate([state[:, :, 1:], wall_rows[:, :, None]], axis=2)
    return x_plus, x_minus, r_plus, r_minus, t_plus, t_minus


def cycle_filter(state, cutoff):
    inner_rows = state[:, :, :NF, :]
    spectrum = jnp.fft.rfft(inner_rows, axis=-1)
    mode_index = jnp.arange(NT // 2 + 1, dtype=jnp.int32)
    kept_modes = mode_index[None, :] < cutoff[:, None]
    spectrum = jnp.where(kept_modes[None, None], spectrum, 0.0)
    filtered = jnp.fft.irfft(spectrum, n=NT, axis=-1).astype(state.dtype)
    return jnp.concatenate([filtered, state[:, :, NF:, :]], axis=2)


def full_rate(state, spacing, angle_step):
    x_plus, x_minus, r_plus, r_minus, t_plus, t_minus = neighbours(state)
    return tendency(state, x_plus, x_minus, r_plus, r_minus, t_plus, t_minus, spacing, angle_step)


def reference(density, velocity, pressure, cutoff):
    spacing = 1.0 / NR
    angle_step = 2.0 * math.pi / NT
    time_step = 0.05 * spacing
    state = jnp.concatenate([density[None], velocity, pressure[None]], axis=0)
    start_state = cycle_filter(state, cutoff)
    section_one = start_state + time_step * full_rate(start_state, spacing, angle_step)
    section_filtered = cycle_filter(section_one, cutoff)
    result = 0.5 * start_state + 0.5 * (section_filtered + time_step * full_rate(section_filtered, spacing, angle_step))
    return result[0], result[1:4], result[4]
```

```python
import functools
import math

import jax
import jax.numpy as jnp
import numpy as np
from jax import lax
from jax.experimental import pallas as pl
from jax.experimental.pallas import tpu as pltpu
from jax.sharding import PartitionSpec as P

MESH = pl.DeviceIdType.MESH
PAD = 8
SUB = 32


def tables(points, local, modes):
    width = -(-(2 * modes - 1) // 128) * 128
    mode = np.zeros(width, np.int64)
    mode[:modes] = np.arange(modes)
    mode[modes : 2 * modes - 1] = np.arange(1, modes)

    def rows(index):
        angle = 2.0 * np.pi / points * ((index[:, None] * mode[None, :]) % points)
        out = np.where(np.arange(width) < modes, np.cos(angle), np.sin(angle))
        out[:, 2 * modes - 1 :] = 0.0
        return out

    sectors = points // local
    forward = rows(np.arange(points)).reshape(sectors, local, width)
    inverse = np.zeros((sectors, width, 2 * local))
    for s in range(sectors):
        inverse[s, :, :local] = forward[s].T
        edges = rows(np.array([s * local - 1, (s + 1) * local]) % points)
        inverse[s, :, local] = edges[0]
        inverse[s, :, 2 * local - 1] = edges[1]
    scale = np.where(mode == 0, 1.0, 2.0) / points
    scale[2 * modes - 1 :] = 0.0
    return (
        forward.astype(np.float32),
        inverse.astype(np.float32),
        mode.astype(np.int32),
        scale.astype(np.float32),
    )


def kernel(
    spacing, angle_step, inner,
    dens, velo, pres, weight, forward, inverse,
    dens_out, velo_out, pres_out,
    start, section, edge, x_low, x_high, gathered, pack, from_left, from_right, inv_r,
    gather_send, gather_recv, x_send, x_recv, t_send, t_recv,
):
    rows, local = dens.shape[1], dens.shape[2]
    chunks = rows // inner
    tau = 0.05 * spacing
    ax, n_ax = lax.axis_index("ax"), lax.axis_size("ax")
    me = lax.axis_index("sec")
    before, after = lax.rem(ax + n_ax - 1, n_ax), lax.rem(ax + 1, n_ax)
    left, right = lax.rem(me + 3, 4), lax.rem(me + 1, 4)
    mate = me + 1 - 2 * lax.rem(me, 2)
    opposite = lax.rem(me + 2, 4)
    far = lax.rem(mate + 2, 4)

    barrier = pltpu.get_barrier_semaphore()
    for target in ({"ax": before}, {"ax": after}, {"sec": mate}, {"sec": opposite}, {"sec": far}):
        pl.semaphore_signal(barrier, inc=1, device_id=target, device_id_type=MESH)
    pl.semaphore_wait(barrier, 5)

    def remote(src, dst, send, recv, target):
        return pltpu.make_async_remote_copy(
            src_ref=src, dst_ref=dst, send_sem=send, recv_sem=recv,
            device_id=target, device_id_type=MESH,
        )

    def x_copies(state, stage, c):
        here, there = pl.ds(PAD + c * inner, inner), pl.ds(c * inner, inner)
        return (
            remote(state.at[:, 0, here], x_high.at[stage, :, there],
                   x_send.at[stage, c, 0], x_recv.at[stage, c, 0], {"ax": before}),
            remote(state.at[:, 1, here], x_low.at[stage, :, there],
                   x_send.at[stage, c, 1], x_recv.at[stage, c, 1], {"ax": after}),
        )

    def t_copies(stage, c):
        return (
            remote(pack.at[stage, c - 1], from_right.at[stage, c - 1],
                   t_send.at[stage, c, 0], t_recv.at[stage, c, 0], {"sec": left}),
            remote(pack.at[stage, c - 1], from_left.at[stage, c - 1],
                   t_send.at[stage, c, 1], t_recv.at[stage, c, 1], {"sec": right}),
        )

    def gather_copies(stage, p):
        own = gathered.at[stage, 0, p]
        arrived = gathered.at[stage, 2, p]
        return (
            remote(own, arrived, gather_send.at[stage, p, 0], gather_recv.at[stage, p, 0],
                   {"sec": opposite}),
            remote(own, gathered.at[stage, 1, p], gather_send.at[stage, p, 1],
                   gather_recv.at[stage, p, 1], {"sec": mate}),
            remote(arrived, gathered.at[stage, 3, p], gather_send.at[stage, p, 2],
                   gather_recv.at[stage, p, 2], {"sec": mate}),
        )

    lane = lax.broadcasted_iota(jnp.int32, (inner, local), 1)

    def send_chunk(state, stage, c):
        for copy in x_copies(state, stage, c):
            copy.start()
        packed = jnp.zeros((inner, local), jnp.float32)
        for f in range(5):
            for p in range(2):
                k = 2 * f + p
                value = state[f, p, PAD + c * inner : PAD + (c + 1) * inner]
                packed = jnp.where(lane == k, pltpu.roll(value, (k + 1) % local, 1), packed)
                packed = jnp.where(lane == 10 + k, pltpu.roll(value, 10 + k, 1), packed)
        pack[stage, c - 1] = packed
        for copy in t_copies(stage, c):
            copy.start()

    def receive_edges(stage, c):
        for copy in t_copies(stage, c):
            copy.wait_recv()
        low, high = from_left[stage, c - 1], from_right[stage, c - 1]
        for f in range(5):
            for p in range(2):
                k = 2 * f + p
                a = pltpu.roll(low, (local - k) % local, 1)
                b = pltpu.roll(high, local - 1 - (10 + k), 1)
                edge[f, p, c * inner : (c + 1) * inner] = jnp.where(lane == 0, a, b)

    def send_inner(stage, p):
        first, second, _ = gather_copies(stage, p)
        first.start()
        second.start()

    def filter_inner(state, stage):
        for p in range(2):
            first, _, third = gather_copies(stage, p)
            first.wait_recv()
            third.start()
        for p in range(2):
            gather_copies(stage, p)[1].wait_recv()
            gather_copies(stage, p)[2].wait_recv()
            coeffs = None
            for slots, owners in (((0, 1), (me, mate)), ((2, 3), (opposite, far))):
                values = jnp.concatenate([gathered[stage, slots[0], p], gathered[stage, slots[1], p]], axis=1)
                basis = jnp.concatenate([forward[owners[0]], forward[owners[1]]], axis=0)
                part = jnp.dot(values, basis, precision=lax.Precision.HIGHEST, preferred_element_type=jnp.float32)
                coeffs = part if coeffs is None else coeffs + part
            coeffs = coeffs.reshape(5, inner, -1) * weight[...][None]
            flat = coeffs.reshape(5 * inner, -1)
            both = jnp.dot(flat, inverse[me], precision=lax.Precision.HIGHEST, preferred_element_type=jnp.float32)
            across = jnp.dot(coeffs[:, :8].reshape(40, -1), inverse[opposite, :, :local],
                             precision=lax.Precision.HIGHEST, preferred_element_type=jnp.float32)
            for f in range(5):
                state[f, p, PAD : PAD + inner] = both[f * inner : (f + 1) * inner, :local]
                edge[f, p, 0:inner] = both[f * inner : (f + 1) * inner, local:]
                row = across[8 * f : 8 * f + 1]
                state[f, p, PAD - 1 : PAD] = -row if f in (2, 3) else row
        for copy in x_copies(state, stage, 0):
            copy.start()

    def wall(state):
        for f in range(5):
            for p in range(2):
                row = state[f, p, PAD + rows - 1 : PAD + rows]
                state[f, p, PAD + rows : PAD + rows + 1] = -row if f == 2 else row

    sub_lane = lax.broadcasted_iota(jnp.int32, (SUB, local), 1)

    def advance(state, stage, p, r0):
        here = slice(PAD + r0, PAD + r0 + SUB)
        plain = slice(r0, r0 + SUB)
        s = [state[f, p, here] for f in range(5)]
        over_r = inv_r[plain]
        over_rho = 1.0 / s[0]
        u, v, w = s[1], s[2], s[3]

        def grads(f):
            if p == 0:
                gx = state[f, 1, here] - x_low[stage, f, plain]
            else:
                gx = x_high[stage, f, plain] - state[f, 0, here]
            gr = state[f, p, PAD + r0 + 1 : PAD + r0 + 1 + SUB] - state[f, p, PAD + r0 - 1 : PAD + r0 - 1 + SUB]
            border = edge[f, p, plain]
            ahead = jnp.where(sub_lane == local - 1, border, pltpu.roll(s[f], local - 1, 1))
            behind = jnp.where(sub_lane == 0, border, pltpu.roll(s[f], 1, 1))
            gt = (ahead - behind) * ((0.5 / angle_step) * over_r)
            return gx * (0.5 / spacing), gr * (0.5 / spacing), gt

        g = [grads(f) for f in range(5)]
        advect = [u * gx + v * gr + w * gt for gx, gr, gt in g]
        diverg = g[1][0] + g[2][1] + v * over_r + g[3][2]
        rates = (
            -advect[0] - s[0] * diverg,
            -advect[1] - g[4][0] * over_rho,
            -advect[2] + w * w * over_r - g[4][1] * over_rho,
            -advect[3] - v * w * over_r - g[4][2] * over_rho,
            -advect[4] - 1.4 * s[4] * diverg,
        )
        return s, [tau * rate for rate in rates]

    for p in range(2):
        for f in range(5):
            source = dens if f == 0 else pres if f == 4 else velo.at[f - 1]
            gathered[0, 0, p, f * inner : (f + 1) * inner] = source[p, 0:inner]
        send_inner(0, p)
    for c in range(1, chunks):
        span = slice(c * inner, (c + 1) * inner)
        for f in range(5):
            source = dens if f == 0 else pres if f == 4 else velo.at[f - 1]
            start[f, :, PAD + c * inner : PAD + (c + 1) * inner] = source[:, span]
        send_chunk(start, 0, c)
    wall(start)
    radius = (lax.broadcasted_iota(jnp.int32, (rows, local), 0).astype(jnp.float32) + 0.5) * spacing
    inv_r[...] = 1.0 / radius
    filter_inner(start, 0)

    order = list(range(1, chunks)) + [0]
    for c in order:
        for copy in x_copies(start, 0, c):
            copy.wait_recv()
        if c > 0:
            receive_edges(0, c)
        for p in range(2):
            for r0 in range(c * inner, (c + 1) * inner, SUB):
                s, step = advance(start, 0, p, r0)
                for f in range(5):
                    if c > 0:
                        section[f, p, PAD + r0 : PAD + r0 + SUB] = s[f] + step[f]
                    else:
                        gathered[1, 0, p, f * inner + r0 : f * inner + r0 + SUB] = s[f] + step[f]
            if c == 0:
                send_inner(1, p)
        if c > 0:
            send_chunk(section, 1, c)
    wall(section)
    filter_inner(section, 1)

    for c in order:
        for copy in x_copies(section, 1, c):
            copy.wait_recv()
        if c > 0:
            receive_edges(1, c)
        for p in range(2):
            for r0 in range(c * inner, (c + 1) * inner, SUB):
                s, step = advance(section, 1, p, r0)
                for f in range(5):
                    value = 0.5 * start[f, p, PAD + r0 : PAD + r0 + SUB] + 0.5 * (s[f] + step[f])
                    target = dens_out if f == 0 else pres_out if f == 4 else velo_out.at[f - 1]
                    target[p, r0 : r0 + SUB] = value

    for stage, state in ((0, start), (1, section)):
        for c in range(chunks):
            for copy in x_copies(state, stage, c):
                copy.wait_send()
            if c > 0:
                for copy in t_copies(stage, c):
                    copy.wait_send()
        for p in range(2):
            for copy in gather_copies(stage, p):
                copy.wait_send()


def body(density, velocity, pressure, cutoff):
    planes, rows, local = density.shape
    points = local * lax.axis_size("sec")
    inner = rows // 4
    forward, inverse, mode, scale = tables(points, local, 2 * inner + 1)
    weight = jnp.where(mode[None, :] < cutoff[:, None], scale[None, :], 0.0).astype(jnp.float32)
    f32 = jnp.float32
    outer_chunks = rows // inner - 1
    vmem = pl.BlockSpec(memory_space=pltpu.VMEM)
    run = pl.pallas_call(
        functools.partial(kernel, 1.0 / rows, 2.0 * math.pi / points, inner),
        out_shape=(
            jax.ShapeDtypeStruct(density.shape, f32),
            jax.ShapeDtypeStruct(velocity.shape, f32),
            jax.ShapeDtypeStruct(pressure.shape, f32),
        ),
        in_specs=[vmem] * 6,
        out_specs=(vmem,) * 3,
        scratch_shapes=[
            pltpu.VMEM((5, planes, rows + 2 * PAD, local), f32),
            pltpu.VMEM((5, planes, rows + 2 * PAD, local), f32),
            pltpu.VMEM((5, planes, rows, local), f32),
            pltpu.VMEM((2, 5, rows, local), f32),
            pltpu.VMEM((2, 5, rows, local), f32),
            pltpu.VMEM((2, 4, planes, 5 * inner, local), f32),
            pltpu.VMEM((2, outer_chunks, inner, local), f32),
            pltpu.VMEM((2, outer_chunks, inner, local), f32),
            pltpu.VMEM((2, outer_chunks, inner, local), f32),
            pltpu.VMEM((rows, local), f32),
            pltpu.SemaphoreType.DMA((2, planes, 3)),
            pltpu.SemaphoreType.DMA((2, planes, 3)),
            pltpu.SemaphoreType.DMA((2, outer_chunks + 1, 2)),
            pltpu.SemaphoreType.DMA((2, outer_chunks + 1, 2)),
            pltpu.SemaphoreType.DMA((2, outer_chunks + 1, 2)),
            pltpu.SemaphoreType.DMA((2, outer_chunks + 1, 2)),
        ],
        compiler_params=pltpu.CompilerParams(
            collective_id=0, has_side_effects=True, vmem_limit_bytes=48 * 1024 * 1024
        ),
    )
    return run(density, velocity, pressure, weight, jnp.asarray(forward), jnp.asarray(inverse))


def solution(mesh):
    return jax.shard_map(
        body,
        mesh=mesh,
        in_specs=(P("ax", None, "sec"), P(None, "ax", None, "sec"), P("ax", None, "sec"), P()),
        out_specs=(P("ax", None, "sec"), P(None, "ax", None, "sec"), P("ax", None, "sec")),
        check_vma=False,
    )
```

```python
import functools
import math

import jax
import jax.numpy as jnp
import numpy as np
from jax import lax
from jax.experimental import pallas as pl
from jax.experimental.pallas import tpu as pltpu
from jax.sharding import PartitionSpec as P

MESH = pl.DeviceIdType.MESH
PAD = 8
SUB = 32


def tables(points, local, modes):
    width = -(-(2 * modes - 1) // 128) * 128
    mode = np.zeros(width, np.int64)
    mode[:modes] = np.arange(modes)
    mode[modes : 2 * modes - 1] = np.arange(1, modes)

    def rows(index):
        angle = 2.0 * np.pi / points * ((index[:, None] * mode[None, :]) % points)
        out = np.where(np.arange(width) < modes, np.cos(angle), np.sin(angle))
        out[:, 2 * modes - 1 :] = 0.0
        return out

    sectors = points // local
    forward = rows(np.arange(points)).reshape(sectors, local, width)
    scale = np.where(mode == 0, 1.0, 2.0) / points
    scale[2 * modes - 1 :] = 0.0
    return (
        forward.astype(np.float32),
        mode.astype(np.int32),
        scale.astype(np.float32),
    )


def kernel(
    spacing, angle_step, inner,
    dens, velo, pres, weight_in, forward_in,
    dens_out, velo_out, pres_out,
    start, section, halo, halo_next, edge, edge_halo, gathered, pack, from_left, from_right, inv_r,
    weight, forward, inverse,
    load_sem, gather_send, gather_recv, x_send, x_recv, mate_send, mate_recv, hop_send, hop_recv,
    t_send, t_recv,
):
    rows, local = inv_r.shape
    chunks = (rows - inner) // SUB
    tau = 0.05 * spacing
    ax, n_ax = lax.axis_index("ax"), lax.axis_size("ax")
    me = lax.axis_index("sec")
    odd = lax.rem(ax, 2)
    before, after = lax.rem(ax + n_ax - 1, n_ax), lax.rem(ax + 1, n_ax)
    ax_mate = ax + 1 - 2 * odd
    hop_to = lax.rem(ax + 2 - 4 * odd + n_ax, n_ax)
    hop_from = lax.rem(ax - 2 + 4 * odd + n_ax, n_ax)
    left, right = lax.rem(me + 3, 4), lax.rem(me + 1, 4)
    mate = me + 1 - 2 * lax.rem(me, 2)
    opposite = lax.rem(me + 2, 4)
    far = lax.rem(mate + 2, 4)

    whole = pl.ds(PAD, rows)
    loads = [
        pltpu.make_async_copy(dens, start.at[0, :, whole], load_sem.at[0]),
        pltpu.make_async_copy(velo, start.at[1:4, :, whole], load_sem.at[1]),
        pltpu.make_async_copy(pres, start.at[4, :, whole], load_sem.at[2]),
        pltpu.make_async_copy(weight_in, weight, load_sem.at[3]),
        pltpu.make_async_copy(forward_in, forward, load_sem.at[4]),
    ]
    for load in loads:
        load.start()

    barrier = pltpu.get_barrier_semaphore()
    for target in (
        {"ax": before}, {"ax": after}, {"ax": hop_to}, {"ax": hop_from},
        {"sec": mate}, {"sec": opposite}, {"sec": far},
    ):
        pl.semaphore_signal(barrier, inc=1, device_id=target, device_id_type=MESH)
    pl.semaphore_wait(barrier, 7)

    def remote(src, dst, send, recv, target):
        return pltpu.make_async_remote_copy(
            src_ref=src, dst_ref=dst, send_sem=send, recv_sem=recv,
            device_id=target, device_id_type=MESH,
        )

    def inner_copies(stage):
        here = pl.ds(PAD, inner)
        if stage == 0:
            state, low, high = start, halo.at[0, :, 1, here], halo.at[1, :, 0, here]
        else:
            state, low, high = section, halo_next.at[0, :, 0:inner], halo_next.at[1, :, 0:inner]
        return (
            remote(state.at[:, 0, here], high, x_send.at[stage, 0], x_recv.at[stage, 0], {"ax": before}),
            remote(state.at[:, 1, here], low, x_send.at[stage, 1], x_recv.at[stage, 1], {"ax": after}),
        )

    def mate_copy(k):
        here = pl.ds(PAD + inner + k * SUB, SUB)
        return remote(start.at[:, :, here], halo.at[odd, :, :, here],
                      mate_send.at[k], mate_recv.at[k], {"ax": ax_mate})

    def hop_copy(k):
        here = pl.ds(PAD + inner + k * SUB, SUB)
        return remote(halo.at[1 - odd, :, :, here], halo.at[odd, :, :, here],
                      hop_send.at[k], hop_recv.at[k], {"ax": hop_to})

    def t_copies(kind, k):
        return (
            remote(pack.at[kind, k], from_right.at[kind, k],
                   t_send.at[kind, k, 0], t_recv.at[kind, k, 0], {"sec": left}),
            remote(pack.at[kind, k], from_left.at[kind, k],
                   t_send.at[kind, k, 1], t_recv.at[kind, k, 1], {"sec": right}),
        )

    def own_copy(stage, p, way):
        return remote(gathered.at[stage, 0, p], gathered.at[stage, 2 - way, p],
                      gather_send.at[stage, p, way], gather_recv.at[stage, p, way],
                      {"sec": mate if way else opposite})

    def pass_copy(stage, p):
        return remote(gathered.at[stage, 2, p], gathered.at[stage, 3, p],
                      gather_send.at[stage, p, 2], gather_recv.at[stage, p, 2], {"sec": mate})

    sub_lane = lax.broadcasted_iota(jnp.int32, (SUB, local), 1)

    def padded(r0, offset=0):
        return slice(PAD + r0 + offset, PAD + r0 + offset + SUB)

    def first_row(k):
        return inner + k * SUB

    def beside(f, q, where):
        return halo[q, f, 1 - q, where]

    def own(state):
        return lambda f, p, where: state[f, p, where]

    def send_edges(get, kind, k):
        packed = jnp.zeros((SUB, local), jnp.float32)
        for f in range(5):
            for p in range(2):
                i = 2 * f + p
                value = get(f, p, padded(first_row(k)))
                packed = jnp.where(sub_lane == i, pltpu.roll(value, (i + 1) % local, 1), packed)
                packed = jnp.where(sub_lane == 10 + i, pltpu.roll(value, 10 + i, 1), packed)
        pack[kind, k] = packed
        for copy in t_copies(kind, k):
            copy.start()

    def receive_edges(target, kind, k):
        for copy in t_copies(kind, k):
            copy.wait_recv()
        low, high = from_left[kind, k], from_right[kind, k]
        r0 = first_row(k)
        for f in range(5):
            for p in range(2):
                i = 2 * f + p
                a = pltpu.roll(low, (local - i) % local, 1)
                b = pltpu.roll(high, local - 1 - (10 + i), 1)
                target[f, p, r0 : r0 + SUB] = jnp.where(sub_lane == 0, a, b)

    def send_inner(stage, p):
        own_copy(stage, p, 0).start()
        own_copy(stage, p, 1).start()

    def pass_inner(stage, p):
        own_copy(stage, p, 0).wait_recv()
        pass_copy(stage, p).start()

    def back(coeffs, basis):
        return lax.dot_general(coeffs, basis, (((1,), (1,)), ((), ())), precision=lax.Precision.HIGHEST,
                               preferred_element_type=jnp.float32)

    def filter_inner(state, stage):
        for p in range(2):
            own_copy(stage, p, 1).wait_recv()
            pass_copy(stage, p).wait_recv()
            coeffs = None
            for slots, owners in (((0, 1), (me, mate)), ((2, 3), (opposite, far))):
                values = jnp.concatenate([gathered[stage, slots[0], p], gathered[stage, slots[1], p]], axis=1)
                basis = jnp.concatenate([forward[owners[0]], forward[owners[1]]], axis=0)
                part = jnp.dot(values, basis, precision=lax.Precision.HIGHEST, preferred_element_type=jnp.float32)
                coeffs = part if coeffs is None else coeffs + part
            coeffs = coeffs.reshape(5, inner, -1) * weight[...][None]
            flat = coeffs.reshape(5 * inner, -1)
            both = back(flat, inverse[...])
            across = back(coeffs[:, :8].reshape(40, -1), forward[opposite])
            for f in range(5):
                state[f, p, PAD : PAD + inner] = both[f * inner : (f + 1) * inner, :local]
                edge[f, p, 0:inner] = both[f * inner : (f + 1) * inner, local:]
                row = across[8 * f : 8 * f + 1]
                state[f, p, PAD - 1 : PAD] = -row if f in (2, 3) else row
            inner_copies(stage)[p].start()

    def wall(get, put):
        for f in range(5):
            for p in range(2):
                row = get(f, p, slice(PAD + rows - 1, PAD + rows))
                put(f, p, slice(PAD + rows, PAD + rows + 1), -row if f == 2 else row)

    def put_start(f, p, where, row):
        start[f, p, where] = row

    def put_section(f, p, where, row):
        section[f, p, where] = row

    def put_beside(f, q, where, row):
        halo[q, f, 1 - q, where] = row

    def advance(get, p, r0, ahead_x, behind_x, border_ref):
        s = [get(f, p, padded(r0)) for f in range(5)]
        over_r = inv_r[r0 : r0 + SUB]
        over_rho = 1.0 / s[0]
        u, v, w = s[1], s[2], s[3]

        def grads(f):
            gx = ahead_x(f) - behind_x(f)
            gr = get(f, p, padded(r0, 1)) - get(f, p, padded(r0, -1))
            border = border_ref[f, p, r0 : r0 + SUB]
            ahead = jnp.where(sub_lane == local - 1, border, pltpu.roll(s[f], local - 1, 1))
            behind = jnp.where(sub_lane == 0, border, pltpu.roll(s[f], 1, 1))
            gt = (ahead - behind) * ((0.5 / angle_step) * over_r)
            return gx * (0.5 / spacing), gr * (0.5 / spacing), gt

        g = [grads(f) for f in range(5)]
        advect = [u * gx + v * gr + w * gt for gx, gr, gt in g]
        diverg = g[1][0] + g[2][1] + v * over_r + g[3][2]
        rates = (
            -advect[0] - s[0] * diverg,
            -advect[1] - g[4][0] * over_rho,
            -advect[2] + w * w * over_r - g[4][1] * over_rho,
            -advect[3] - v * w * over_r - g[4][2] * over_rho,
            -advect[4] - 1.4 * s[4] * diverg,
        )
        return s, [tau * rate for rate in rates]

    def advance_start(p, r0):
        here = padded(r0)
        if p == 0:
            ahead, behind = (lambda f: start[f, 1, here]), (lambda f: halo[0, f, 1, here])
        else:
            ahead, behind = (lambda f: halo[1, f, 0, here]), (lambda f: start[f, 0, here])
        return advance(own(start), p, r0, ahead, behind, edge)

    def advance_beside(q, r0):
        here = padded(r0)
        if q == 0:
            ahead, behind = (lambda f: start[f, 0, here]), (lambda f: halo[0, f, 0, here])
        else:
            ahead, behind = (lambda f: halo[1, f, 1, here]), (lambda f: start[f, 1, here])
        return advance(beside, q, r0, ahead, behind, edge_halo)

    def finish(p, r0):
        here, plain = padded(r0), slice(r0, r0 + SUB)
        if p == 0:
            ahead, behind = (lambda f: section[f, 1, here]), (lambda f: halo_next[0, f, plain])
        else:
            ahead, behind = (lambda f: halo_next[1, f, plain]), (lambda f: section[f, 0, here])
        s, step = advance(own(section), p, r0, ahead, behind, edge)
        for f in range(5):
            value = 0.5 * start[f, p, here] + 0.5 * (s[f] + step[f])
            target = dens_out if f == 0 else pres_out if f == 4 else velo_out.at[f - 1]
            target[p, plain] = value

    def pass_chunk(k):
        mate_copy(k).wait_recv()
        hop_copy(k).start()

    def take_chunk(k):
        hop_copy(k).wait_recv()
        send_edges(beside, 1, k)
        receive_edges(edge, 0, k)
        r0 = first_row(k)
        for p in range(2):
            s, step = advance_start(p, r0)
            for f in range(5):
                section[f, p, padded(r0)] = s[f] + step[f]
        send_edges(own(section), 2, k)

    def take_beside(k):
        receive_edges(edge_halo, 1, k)
        r0 = first_row(k)
        for q in range(2):
            s, step = advance_beside(q, r0)
            for f in range(5):
                halo_next[q, f, r0 : r0 + SUB] = s[f] + step[f]

    for load in loads[:3]:
        load.wait()
    for p in range(2):
        for f in range(5):
            gathered[0, 0, p, f * inner : (f + 1) * inner] = start[f, p, PAD : PAD + inner]
        send_inner(0, p)
    for k in range(chunks):
        mate_copy(k).start()
    for k in range(chunks):
        send_edges(own(start), 0, k)
    wall(own(start), put_start)
    radius = (lax.broadcasted_iota(jnp.int32, (rows, local), 0).astype(jnp.float32) + 0.5) * spacing
    inv_r[...] = 1.0 / radius
    for load in loads[3:]:
        load.wait()
    inverse[0:local] = forward[me]
    inverse[local : 2 * local] = jnp.zeros((local, inverse.shape[1]), jnp.float32)
    inverse[local : local + 1] = forward[left, local - 1 : local]
    inverse[2 * local - 1 : 2 * local] = forward[right, 0:1]
    for p in range(2):
        pass_inner(0, p)
        pass_chunk(p)
    filter_inner(start, 0)

    for k in range(2, chunks):
        pass_chunk(k)
        take_chunk(k - 2)
    take_chunk(chunks - 2)
    for copy in inner_copies(0):
        copy.wait_recv()
    for p in range(2):
        for r0 in range(0, inner, SUB):
            s, step = advance_start(p, r0)
            for f in range(5):
                gathered[1, 0, p, f * inner + r0 : f * inner + r0 + SUB] = s[f] + step[f]
        send_inner(1, p)
    for k in range(chunks - 2):
        take_beside(k)
    for p in range(2):
        pass_inner(1, p)
    take_chunk(chunks - 1)
    wall(beside, put_beside)
    wall(own(section), put_section)
    for k in range(chunks - 2, chunks):
        take_beside(k)
    filter_inner(section, 1)

    for k in range(chunks):
        receive_edges(edge, 2, k)
        for p in range(2):
            finish(p, first_row(k))
    for copy in inner_copies(1):
        copy.wait_recv()
    for p in range(2):
        for r0 in range(0, inner, SUB):
            finish(p, r0)

    for k in range(chunks):
        mate_copy(k).wait_send()
        hop_copy(k).wait_send()
        for kind in range(3):
            for copy in t_copies(kind, k):
                copy.wait_send()
    for stage in range(2):
        for copy in inner_copies(stage):
            copy.wait_send()
        for p in range(2):
            own_copy(stage, p, 0).wait_send()
            own_copy(stage, p, 1).wait_send()
            pass_copy(stage, p).wait_send()


def body(density, velocity, pressure, cutoff):
    planes, rows, local = density.shape
    points = local * lax.axis_size("sec")
    inner = rows // 4
    forward, mode, scale = tables(points, local, 2 * inner + 1)
    weight = jnp.where(mode[None, :] < cutoff[:, None], scale[None, :], 0.0).astype(jnp.float32)
    f32 = jnp.float32
    chunks = (rows - inner) // SUB
    vmem = pl.BlockSpec(memory_space=pltpu.VMEM)
    hbm = pl.BlockSpec(memory_space=pltpu.MemorySpace.HBM)
    run = pl.pallas_call(
        functools.partial(kernel, 1.0 / rows, 2.0 * math.pi / points, inner),
        out_shape=(
            jax.ShapeDtypeStruct(density.shape, f32),
            jax.ShapeDtypeStruct(velocity.shape, f32),
            jax.ShapeDtypeStruct(pressure.shape, f32),
        ),
        in_specs=[hbm] * 5,
        out_specs=(vmem,) * 3,
        scratch_shapes=[
            pltpu.VMEM((5, planes, rows + 2 * PAD, local), f32),
            pltpu.VMEM((5, planes, rows + 2 * PAD, local), f32),
            pltpu.VMEM((2, 5, planes, rows + 2 * PAD, local), f32),
            pltpu.VMEM((2, 5, rows, local), f32),
            pltpu.VMEM((5, planes, rows, local), f32),
            pltpu.VMEM((5, 2, rows, local), f32),
            pltpu.VMEM((2, 4, planes, 5 * inner, local), f32),
            pltpu.VMEM((3, chunks, SUB, local), f32),
            pltpu.VMEM((3, chunks, SUB, local), f32),
            pltpu.VMEM((3, chunks, SUB, local), f32),
            pltpu.VMEM((rows, local), f32),
            pltpu.VMEM(weight.shape, f32),
            pltpu.VMEM(forward.shape, f32),
            pltpu.VMEM((2 * local, forward.shape[2]), f32),
            pltpu.SemaphoreType.DMA((5,)),
            pltpu.SemaphoreType.DMA((2, planes, 3)),
            pltpu.SemaphoreType.DMA((2, planes, 3)),
            pltpu.SemaphoreType.DMA((2, 2)),
            pltpu.SemaphoreType.DMA((2, 2)),
            pltpu.SemaphoreType.DMA((chunks,)),
            pltpu.SemaphoreType.DMA((chunks,)),
            pltpu.SemaphoreType.DMA((chunks,)),
            pltpu.SemaphoreType.DMA((chunks,)),
            pltpu.SemaphoreType.DMA((3, chunks, 2)),
            pltpu.SemaphoreType.DMA((3, chunks, 2)),
        ],
        compiler_params=pltpu.CompilerParams(
            collective_id=0, has_side_effects=True, vmem_limit_bytes=62 * 1024 * 1024
        ),
    )
    return run(density, velocity, pressure, weight, jnp.asarray(forward))


def solution(mesh):
    return jax.shard_map(
        body,
        mesh=mesh,
        in_specs=(P("ax", None, "sec"), P(None, "ax", None, "sec"), P("ax", None, "sec"), P()),
        out_specs=(P("ax", None, "sec"), P(None, "ax", None, "sec"), P("ax", None, "sec")),
        check_vma=False,
    )
```

```python
import functools
import math

import jax
import jax.numpy as jnp
import numpy as np
from jax import lax
from jax.experimental import pallas as pl
from jax.experimental.pallas import tpu as pltpu
from jax.sharding import PartitionSpec as P

MESH = pl.DeviceIdType.MESH
PAD = 8
SUB = 32


def tables(points, local, modes):
    width = -(-(2 * modes - 1) // 128) * 128
    mode = np.zeros(width, np.int64)
    mode[:modes] = np.arange(modes)
    mode[modes : 2 * modes - 1] = np.arange(1, modes)

    def rows(index):
        angle = 2.0 * np.pi / points * ((index[:, None] * mode[None, :]) % points)
        out = np.where(np.arange(width) < modes, np.cos(angle), np.sin(angle))
        out[:, 2 * modes - 1 :] = 0.0
        return out

    sectors = points // local
    forward = rows(np.arange(points)).reshape(sectors, local, width)
    return forward.astype(np.float32)


def kernel(
    spacing, angle_step, inner,
    dens, velo, pres, cutoff, forward_in,
    dens_out, velo_out, pres_out,
    start, section, halo, halo_next, edge, edge_halo, gathered, pack, from_left, from_right, inv_r,
    weight, forward, inverse,
    load_sem, gather_send, gather_recv, x_send, x_recv, mate_send, mate_recv, hop_send, hop_recv,
    t_send, t_recv,
):
    rows, local = inv_r.shape
    chunks = (rows - inner) // SUB
    tau = 0.05 * spacing
    ax, n_ax = lax.axis_index("ax"), lax.axis_size("ax")
    me = lax.axis_index("sec")
    odd = lax.rem(ax, 2)
    before, after = lax.rem(ax + n_ax - 1, n_ax), lax.rem(ax + 1, n_ax)
    ax_mate = ax + 1 - 2 * odd
    hop_to = lax.rem(ax + 2 - 4 * odd + n_ax, n_ax)
    hop_from = lax.rem(ax - 2 + 4 * odd + n_ax, n_ax)
    left, right = lax.rem(me + 3, 4), lax.rem(me + 1, 4)
    mate = me + 1 - 2 * lax.rem(me, 2)
    opposite = lax.rem(me + 2, 4)
    far = lax.rem(mate + 2, 4)

    whole = pl.ds(PAD, rows)
    loads = [
        pltpu.make_async_copy(dens, start.at[0, :, whole], load_sem.at[0]),
        pltpu.make_async_copy(velo, start.at[1:4, :, whole], load_sem.at[1]),
        pltpu.make_async_copy(pres, start.at[4, :, whole], load_sem.at[2]),
        pltpu.make_async_copy(forward_in, forward, load_sem.at[3]),
    ]
    for load in loads:
        load.start()

    barrier = pltpu.get_barrier_semaphore()
    for target in (
        {"ax": before}, {"ax": after}, {"ax": hop_to}, {"ax": hop_from},
        {"sec": mate}, {"sec": opposite}, {"sec": far},
    ):
        pl.semaphore_signal(barrier, inc=1, device_id=target, device_id_type=MESH)
    pl.semaphore_wait(barrier, 7)

    def remote(src, dst, send, recv, target):
        return pltpu.make_async_remote_copy(
            src_ref=src, dst_ref=dst, send_sem=send, recv_sem=recv,
            device_id=target, device_id_type=MESH,
        )

    def inner_copies(stage):
        here = pl.ds(PAD, inner)
        if stage == 0:
            state, low, high = start, halo.at[0, :, 1, here], halo.at[1, :, 0, here]
        else:
            state, low, high = section, halo_next.at[0, :, 0:inner], halo_next.at[1, :, 0:inner]
        return (
            remote(state.at[:, 0, here], high, x_send.at[stage, 0], x_recv.at[stage, 0], {"ax": before}),
            remote(state.at[:, 1, here], low, x_send.at[stage, 1], x_recv.at[stage, 1], {"ax": after}),
        )

    def mate_copy(k):
        here = pl.ds(PAD + inner + k * SUB, SUB)
        return remote(start.at[:, :, here], halo.at[odd, :, :, here],
                      mate_send.at[k], mate_recv.at[k], {"ax": ax_mate})

    def hop_copy(k):
        here = pl.ds(PAD + inner + k * SUB, SUB)
        return remote(halo.at[1 - odd, :, :, here], halo.at[odd, :, :, here],
                      hop_send.at[k], hop_recv.at[k], {"ax": hop_to})

    def t_copies(kind, k):
        return (
            remote(pack.at[kind, k], from_right.at[kind, k],
                   t_send.at[kind, k, 0], t_recv.at[kind, k, 0], {"sec": left}),
            remote(pack.at[kind, k], from_left.at[kind, k],
                   t_send.at[kind, k, 1], t_recv.at[kind, k, 1], {"sec": right}),
        )

    def own_copy(stage, p, way):
        return remote(gathered.at[stage, 0, p], gathered.at[stage, 2 - way, p],
                      gather_send.at[stage, p, way], gather_recv.at[stage, p, way],
                      {"sec": mate if way else opposite})

    def pass_copy(stage, p):
        return remote(gathered.at[stage, 2, p], gathered.at[stage, 3, p],
                      gather_send.at[stage, p, 2], gather_recv.at[stage, p, 2], {"sec": mate})

    sub_lane = lax.broadcasted_iota(jnp.int32, (SUB, local), 1)

    def padded(r0, offset=0):
        return slice(PAD + r0 + offset, PAD + r0 + offset + SUB)

    def first_row(k):
        return inner + k * SUB

    def beside(f, q, where):
        return halo[q, f, 1 - q, where]

    def own(state):
        return lambda f, p, where: state[f, p, where]

    def send_edges(get, kind, k):
        packed = jnp.zeros((SUB, local), jnp.float32)
        for f in range(5):
            for p in range(2):
                i = 2 * f + p
                value = get(f, p, padded(first_row(k)))
                packed = jnp.where(sub_lane == i, pltpu.roll(value, (i + 1) % local, 1), packed)
                packed = jnp.where(sub_lane == 10 + i, pltpu.roll(value, 10 + i, 1), packed)
        pack[kind, k] = packed
        for copy in t_copies(kind, k):
            copy.start()

    def receive_edges(target, kind, k):
        for copy in t_copies(kind, k):
            copy.wait_recv()
        low, high = from_left[kind, k], from_right[kind, k]
        r0 = first_row(k)
        for f in range(5):
            for p in range(2):
                i = 2 * f + p
                a = pltpu.roll(low, (local - i) % local, 1)
                b = pltpu.roll(high, local - 1 - (10 + i), 1)
                target[f, p, r0 : r0 + SUB] = jnp.where(sub_lane == 0, a, b)

    def send_inner(stage, p):
        own_copy(stage, p, 0).start()
        own_copy(stage, p, 1).start()

    def pass_inner(stage, p):
        own_copy(stage, p, 0).wait_recv()
        pass_copy(stage, p).start()

    def back(coeffs, basis):
        return lax.dot_general(coeffs, basis, (((1,), (1,)), ((), ())), precision=lax.Precision.HIGHEST,
                               preferred_element_type=jnp.float32)

    def filter_inner(state, stage):
        for p in range(2):
            own_copy(stage, p, 1).wait_recv()
            pass_copy(stage, p).wait_recv()
            coeffs = None
            for slots, owners in (((0, 1), (me, mate)), ((2, 3), (opposite, far))):
                values = jnp.concatenate([gathered[stage, slots[0], p], gathered[stage, slots[1], p]], axis=1)
                basis = jnp.concatenate([forward[owners[0]], forward[owners[1]]], axis=0)
                part = jnp.dot(values, basis, precision=lax.Precision.HIGHEST, preferred_element_type=jnp.float32)
                coeffs = part if coeffs is None else coeffs + part
            coeffs = coeffs.reshape(5, inner, -1) * weight[...][None]
            flat = coeffs.reshape(5 * inner, -1)
            both = back(flat, inverse[...])
            across = back(coeffs[:, :8].reshape(40, -1), forward[opposite])
            for f in range(5):
                state[f, p, PAD : PAD + inner] = both[f * inner : (f + 1) * inner, :local]
                edge[f, p, 0:inner] = both[f * inner : (f + 1) * inner, local:]
                row = across[8 * f : 8 * f + 1]
                state[f, p, PAD - 1 : PAD] = -row if f in (2, 3) else row
            inner_copies(stage)[p].start()

    def wall(get, put):
        for f in range(5):
            for p in range(2):
                row = get(f, p, slice(PAD + rows - 1, PAD + rows))
                put(f, p, slice(PAD + rows, PAD + rows + 1), -row if f == 2 else row)

    def put_start(f, p, where, row):
        start[f, p, where] = row

    def put_section(f, p, where, row):
        section[f, p, where] = row

    def put_beside(f, q, where, row):
        halo[q, f, 1 - q, where] = row

    def advance(get, p, r0, ahead_x, behind_x, border_ref):
        s = [get(f, p, padded(r0)) for f in range(5)]
        over_r = inv_r[r0 : r0 + SUB]
        over_rho = 1.0 / s[0]
        u, v, w = s[1], s[2], s[3]

        def grads(f):
            gx = ahead_x(f) - behind_x(f)
            gr = get(f, p, padded(r0, 1)) - get(f, p, padded(r0, -1))
            border = border_ref[f, p, r0 : r0 + SUB]
            ahead = jnp.where(sub_lane == local - 1, border, pltpu.roll(s[f], local - 1, 1))
            behind = jnp.where(sub_lane == 0, border, pltpu.roll(s[f], 1, 1))
            gt = (ahead - behind) * ((0.5 / angle_step) * over_r)
            return gx * (0.5 / spacing), gr * (0.5 / spacing), gt

        g = [grads(f) for f in range(5)]
        advect = [u * gx + v * gr + w * gt for gx, gr, gt in g]
        diverg = g[1][0] + g[2][1] + v * over_r + g[3][2]
        rates = (
            -advect[0] - s[0] * diverg,
            -advect[1] - g[4][0] * over_rho,
            -advect[2] + w * w * over_r - g[4][1] * over_rho,
            -advect[3] - v * w * over_r - g[4][2] * over_rho,
            -advect[4] - 1.4 * s[4] * diverg,
        )
        return s, [tau * rate for rate in rates]

    def advance_start(p, r0):
        here = padded(r0)
        if p == 0:
            ahead, behind = (lambda f: start[f, 1, here]), (lambda f: halo[0, f, 1, here])
        else:
            ahead, behind = (lambda f: halo[1, f, 0, here]), (lambda f: start[f, 0, here])
        return advance(own(start), p, r0, ahead, behind, edge)

    def advance_beside(q, r0):
        here = padded(r0)
        if q == 0:
            ahead, behind = (lambda f: start[f, 0, here]), (lambda f: halo[0, f, 0, here])
        else:
            ahead, behind = (lambda f: halo[1, f, 1, here]), (lambda f: start[f, 1, here])
        return advance(beside, q, r0, ahead, behind, edge_halo)

    def finish(p, r0):
        here, plain = padded(r0), slice(r0, r0 + SUB)
        if p == 0:
            ahead, behind = (lambda f: section[f, 1, here]), (lambda f: halo_next[0, f, plain])
        else:
            ahead, behind = (lambda f: halo_next[1, f, plain]), (lambda f: section[f, 0, here])
        s, step = advance(own(section), p, r0, ahead, behind, edge)
        for f in range(5):
            value = 0.5 * start[f, p, here] + 0.5 * (s[f] + step[f])
            target = dens_out if f == 0 else pres_out if f == 4 else velo_out.at[f - 1]
            target[p, plain] = value

    def pass_chunk(k):
        mate_copy(k).wait_recv()
        hop_copy(k).start()

    def take_chunk(k):
        hop_copy(k).wait_recv()
        send_edges(beside, 1, k)
        receive_edges(edge, 0, k)
        r0 = first_row(k)
        for p in range(2):
            s, step = advance_start(p, r0)
            for f in range(5):
                section[f, p, padded(r0)] = s[f] + step[f]
        send_edges(own(section), 2, k)

    def take_beside(k):
        receive_edges(edge_halo, 1, k)
        r0 = first_row(k)
        for q in range(2):
            s, step = advance_beside(q, r0)
            for f in range(5):
                halo_next[q, f, r0 : r0 + SUB] = s[f] + step[f]

    for load in loads[:3]:
        load.wait()
    for p in range(2):
        for f in range(5):
            gathered[0, 0, p, f * inner : (f + 1) * inner] = start[f, p, PAD : PAD + inner]
        send_inner(0, p)
    early = chunks // 2
    for k in range(early):
        mate_copy(k).start()
    wall(own(start), put_start)
    radius = (lax.broadcasted_iota(jnp.int32, (rows, local), 0).astype(jnp.float32) + 0.5) * spacing
    inv_r[...] = 1.0 / radius
    loads[3].wait()
    inverse[0:local] = forward[me]
    inverse[local : 2 * local] = jnp.zeros((local, inverse.shape[1]), jnp.float32)
    inverse[local : local + 1] = forward[left, local - 1 : local]
    inverse[2 * local - 1 : 2 * local] = forward[right, 0:1]
    modes = 2 * inner + 1
    column = lax.broadcasted_iota(jnp.int32, (1, weight.shape[1]), 1)
    mode = jnp.where(column < modes, column, column - (modes - 1))
    scale = jnp.where(column == 0, 1.0 / (4 * local), 2.0 / (4 * local))
    scale = jnp.where(column < 2 * modes - 1, scale, 0.0)
    for j in range(inner):
        weight[j : j + 1] = jnp.where(mode < cutoff[j], scale, 0.0)
    for p in range(2):
        pass_inner(0, p)
        pass_chunk(p)
    for k in range(chunks):
        send_edges(own(start), 0, k)
    filter_inner(start, 0)
    for k in range(early, chunks):
        mate_copy(k).start()

    for k in range(2, early):
        pass_chunk(k)
    for k in range(early):
        take_chunk(k)
    for copy in inner_copies(0):
        copy.wait_recv()
    for p in range(2):
        for r0 in range(0, inner, SUB):
            s, step = advance_start(p, r0)
            for f in range(5):
                gathered[1, 0, p, f * inner + r0 : f * inner + r0 + SUB] = s[f] + step[f]
        send_inner(1, p)
    for k in range(early - 1):
        take_beside(k)
    pass_chunk(early)
    for p in range(2):
        pass_inner(1, p)
        if early + 1 + p < chunks - 1:
            pass_chunk(early + 1 + p)
    filter_inner(section, 1)
    pass_chunk(chunks - 1)
    for k in range(early, chunks):
        take_chunk(k)
    wall(beside, put_beside)
    wall(own(section), put_section)
    for k in range(early - 1, chunks):
        take_beside(k)

    for k in range(chunks):
        receive_edges(edge, 2, k)
        for p in range(2):
            finish(p, first_row(k))
    for copy in inner_copies(1):
        copy.wait_recv()
    for p in range(2):
        for r0 in range(0, inner, SUB):
            finish(p, r0)

    for k in range(chunks):
        mate_copy(k).wait_send()
        hop_copy(k).wait_send()
        for kind in range(3):
            for copy in t_copies(kind, k):
                copy.wait_send()
    for stage in range(2):
        for copy in inner_copies(stage):
            copy.wait_send()
        for p in range(2):
            own_copy(stage, p, 0).wait_send()
            own_copy(stage, p, 1).wait_send()
            pass_copy(stage, p).wait_send()


def body(density, velocity, pressure, cutoff):
    planes, rows, local = density.shape
    points = local * lax.axis_size("sec")
    inner = rows // 4
    forward = tables(points, local, 2 * inner + 1)
    f32 = jnp.float32
    chunks = (rows - inner) // SUB
    vmem = pl.BlockSpec(memory_space=pltpu.VMEM)
    hbm = pl.BlockSpec(memory_space=pltpu.MemorySpace.HBM)
    run = pl.pallas_call(
        functools.partial(kernel, 1.0 / rows, 2.0 * math.pi / points, inner),
        out_shape=(
            jax.ShapeDtypeStruct(density.shape, f32),
            jax.ShapeDtypeStruct(velocity.shape, f32),
            jax.ShapeDtypeStruct(pressure.shape, f32),
        ),
        in_specs=[hbm] * 3 + [pl.BlockSpec(memory_space=pltpu.SMEM), hbm],
        out_specs=(vmem,) * 3,
        scratch_shapes=[
            pltpu.VMEM((5, planes, rows + 2 * PAD, local), f32),
            pltpu.VMEM((5, planes, rows + 2 * PAD, local), f32),
            pltpu.VMEM((2, 5, planes, rows + 2 * PAD, local), f32),
            pltpu.VMEM((2, 5, rows, local), f32),
            pltpu.VMEM((5, planes, rows, local), f32),
            pltpu.VMEM((5, 2, rows, local), f32),
            pltpu.VMEM((2, 4, planes, 5 * inner, local), f32),
            pltpu.VMEM((3, chunks, SUB, local), f32),
            pltpu.VMEM((3, chunks, SUB, local), f32),
            pltpu.VMEM((3, chunks, SUB, local), f32),
            pltpu.VMEM((rows, local), f32),
            pltpu.VMEM((inner, forward.shape[2]), f32),
            pltpu.VMEM(forward.shape, f32),
            pltpu.VMEM((2 * local, forward.shape[2]), f32),
            pltpu.SemaphoreType.DMA((4,)),
            pltpu.SemaphoreType.DMA((2, planes, 3)),
            pltpu.SemaphoreType.DMA((2, planes, 3)),
            pltpu.SemaphoreType.DMA((2, 2)),
            pltpu.SemaphoreType.DMA((2, 2)),
            pltpu.SemaphoreType.DMA((chunks,)),
            pltpu.SemaphoreType.DMA((chunks,)),
            pltpu.SemaphoreType.DMA((chunks,)),
            pltpu.SemaphoreType.DMA((chunks,)),
            pltpu.SemaphoreType.DMA((3, chunks, 2)),
            pltpu.SemaphoreType.DMA((3, chunks, 2)),
        ],
        compiler_params=pltpu.CompilerParams(
            collective_id=0, has_side_effects=True, vmem_limit_bytes=62 * 1024 * 1024
        ),
    )
    return run(density, velocity, pressure, cutoff, jnp.asarray(forward))


def solution(mesh):
    return jax.shard_map(
        body,
        mesh=mesh,
        in_specs=(P("ax", None, "sec"), P(None, "ax", None, "sec"), P("ax", None, "sec"), P()),
        out_specs=(P("ax", None, "sec"), P(None, "ax", None, "sec"), P("ax", None, "sec")),
        check_vma=False,
    )
```

```python
import functools
import math

import jax
import jax.numpy as jnp
import numpy as np
from jax import lax
from jax.experimental import pallas as pl
from jax.experimental.pallas import tpu as pltpu
from jax.sharding import PartitionSpec as P

MESH = pl.DeviceIdType.MESH
PAD = 8
SUB = 32


def tables(points, local, modes):
    width = -(-(2 * modes - 1) // 128) * 128
    mode = np.zeros(width, np.int64)
    mode[:modes] = np.arange(modes)
    mode[modes : 2 * modes - 1] = np.arange(1, modes)

    def rows(index):
        angle = 2.0 * np.pi / points * ((index[:, None] * mode[None, :]) % points)
        out = np.where(np.arange(width) < modes, np.cos(angle), np.sin(angle))
        out[:, 2 * modes - 1 :] = 0.0
        return out

    sectors = points // local
    forward = rows(np.arange(points)).reshape(sectors, local, width)
    return forward.astype(np.float32)


def kernel(
    spacing, angle_step, inner,
    dens, velo, pres, cutoff, forward_in,
    dens_out, velo_out, pres_out,
    start, section, halo, halo_next, edge, edge_halo, gathered, pack, from_left, from_right, inv_r,
    weight, forward, inverse, basis_high, basis_low, inverse_high, inverse_low,
    load_sem, gather_send, gather_recv, x_send, x_recv, mate_send, mate_recv, hop_send, hop_recv,
    t_send, t_recv,
):
    rows, local = inv_r.shape
    chunks = (rows - inner) // SUB
    tau = 0.05 * spacing
    ax, n_ax = lax.axis_index("ax"), lax.axis_size("ax")
    me = lax.axis_index("sec")
    odd = lax.rem(ax, 2)
    before, after = lax.rem(ax + n_ax - 1, n_ax), lax.rem(ax + 1, n_ax)
    ax_mate = ax + 1 - 2 * odd
    hop_to = lax.rem(ax + 2 - 4 * odd + n_ax, n_ax)
    hop_from = lax.rem(ax - 2 + 4 * odd + n_ax, n_ax)
    left, right = lax.rem(me + 3, 4), lax.rem(me + 1, 4)
    mate = me + 1 - 2 * lax.rem(me, 2)
    opposite = lax.rem(me + 2, 4)
    far = lax.rem(mate + 2, 4)

    whole = pl.ds(PAD, rows)
    loads = [
        pltpu.make_async_copy(dens, start.at[0, :, whole], load_sem.at[0]),
        pltpu.make_async_copy(velo, start.at[1:4, :, whole], load_sem.at[1]),
        pltpu.make_async_copy(pres, start.at[4, :, whole], load_sem.at[2]),
        pltpu.make_async_copy(forward_in, forward, load_sem.at[3]),
    ]
    for load in loads:
        load.start()

    barrier = pltpu.get_barrier_semaphore()
    for target in (
        {"ax": before}, {"ax": after}, {"ax": hop_to}, {"ax": hop_from},
        {"sec": mate}, {"sec": opposite}, {"sec": far},
    ):
        pl.semaphore_signal(barrier, inc=1, device_id=target, device_id_type=MESH)
    pl.semaphore_wait(barrier, 7)

    def remote(src, dst, send, recv, target):
        return pltpu.make_async_remote_copy(
            src_ref=src, dst_ref=dst, send_sem=send, recv_sem=recv,
            device_id=target, device_id_type=MESH,
        )

    def inner_copies(stage):
        here = pl.ds(PAD, inner)
        if stage == 0:
            state, low, high = start, halo.at[0, :, 1, here], halo.at[1, :, 0, here]
        else:
            state, low, high = section, halo_next.at[0, :, 0:inner], halo_next.at[1, :, 0:inner]
        return (
            remote(state.at[:, 0, here], high, x_send.at[stage, 0], x_recv.at[stage, 0], {"ax": before}),
            remote(state.at[:, 1, here], low, x_send.at[stage, 1], x_recv.at[stage, 1], {"ax": after}),
        )

    def mate_copy(k):
        here = pl.ds(PAD + inner + k * SUB, SUB)
        return remote(start.at[:, :, here], halo.at[odd, :, :, here],
                      mate_send.at[k], mate_recv.at[k], {"ax": ax_mate})

    def hop_copy(k):
        here = pl.ds(PAD + inner + k * SUB, SUB)
        return remote(halo.at[1 - odd, :, :, here], halo.at[odd, :, :, here],
                      hop_send.at[k], hop_recv.at[k], {"ax": hop_to})

    def t_copies(kind, k):
        return (
            remote(pack.at[kind, k], from_right.at[kind, k],
                   t_send.at[kind, k, 0], t_recv.at[kind, k, 0], {"sec": left}),
            remote(pack.at[kind, k], from_left.at[kind, k],
                   t_send.at[kind, k, 1], t_recv.at[kind, k, 1], {"sec": right}),
        )

    def own_copy(stage, p, way):
        return remote(gathered.at[stage, 0, p], gathered.at[stage, 2 - way, p],
                      gather_send.at[stage, p, way], gather_recv.at[stage, p, way],
                      {"sec": mate if way else opposite})

    def pass_copy(stage, p):
        return remote(gathered.at[stage, 2, p], gathered.at[stage, 3, p],
                      gather_send.at[stage, p, 2], gather_recv.at[stage, p, 2], {"sec": mate})

    sub_lane = lax.broadcasted_iota(jnp.int32, (SUB, local), 1)

    def padded(r0, offset=0):
        return slice(PAD + r0 + offset, PAD + r0 + offset + SUB)

    def first_row(k):
        return inner + k * SUB

    def beside(f, q, where):
        return halo[q, f, 1 - q, where]

    def own(state):
        return lambda f, p, where: state[f, p, where]

    def send_edges(get, kind, k):
        packed = jnp.zeros((SUB, local), jnp.float32)
        for f in range(5):
            for p in range(2):
                i = 2 * f + p
                value = get(f, p, padded(first_row(k)))
                packed = jnp.where(sub_lane == i, pltpu.roll(value, (i + 1) % local, 1), packed)
                packed = jnp.where(sub_lane == 10 + i, pltpu.roll(value, 10 + i, 1), packed)
        folded = packed[0:8]
        for g in range(1, SUB // 8):
            folded = folded + pltpu.roll(packed[8 * g : 8 * g + 8], 32 * g, 1)
        pack[kind, k] = folded
        for copy in t_copies(kind, k):
            copy.start()

    def unfolded(value):
        parts = [value] + [pltpu.roll(value, local - 32 * g, 1) for g in range(1, SUB // 8)]
        return jnp.concatenate(parts, axis=0)

    def receive_edges(target, kind, k):
        for copy in t_copies(kind, k):
            copy.wait_recv()
        low, high = unfolded(from_left[kind, k]), unfolded(from_right[kind, k])
        r0 = first_row(k)
        for f in range(5):
            for p in range(2):
                i = 2 * f + p
                a = pltpu.roll(low, (local - i) % local, 1)
                b = pltpu.roll(high, local - 1 - (10 + i), 1)
                target[f, p, r0 : r0 + SUB] = jnp.where(sub_lane == 0, a, b)

    def send_inner(stage, p):
        own_copy(stage, p, 0).start()
        own_copy(stage, p, 1).start()

    def pass_inner(stage, p):
        own_copy(stage, p, 0).wait_recv()
        pass_copy(stage, p).start()

    def halves(value):
        high = value.astype(jnp.bfloat16)
        return high, (value - high.astype(jnp.float32)).astype(jnp.bfloat16)

    def product(value, basis_high, basis_low, dim):
        high, low = halves(value)

        def dot(a, b):
            return lax.dot_general(a, b, (((1,), (dim,)), ((), ())), preferred_element_type=jnp.float32)

        return dot(high, basis_high) + (dot(high, basis_low) + dot(low, basis_high))

    def filter_inner(state, stage):
        for p in range(2):
            own_copy(stage, p, 1).wait_recv()
            pass_copy(stage, p).wait_recv()
            values = jnp.concatenate([gathered[stage, slot, p] for slot in range(4)], axis=1)
            coeffs = product(values, basis_high[...], basis_low[...], 0)
            coeffs = coeffs.reshape(5, inner, -1) * weight[...][None]
            flat = coeffs.reshape(5 * inner, -1)
            both = product(flat, inverse_high[...], inverse_low[...], 1)
            across = product(coeffs[:, :8].reshape(40, -1), basis_high[2 * local : 3 * local],
                             basis_low[2 * local : 3 * local], 1)
            for f in range(5):
                state[f, p, PAD : PAD + inner] = both[f * inner : (f + 1) * inner, :local]
                edge[f, p, 0:inner] = both[f * inner : (f + 1) * inner, local:]
                row = across[8 * f : 8 * f + 1]
                state[f, p, PAD - 1 : PAD] = -row if f in (2, 3) else row
            inner_copies(stage)[p].start()

    def wall(get, put):
        for f in range(5):
            for p in range(2):
                row = get(f, p, slice(PAD + rows - 1, PAD + rows))
                put(f, p, slice(PAD + rows, PAD + rows + 1), -row if f == 2 else row)

    def put_start(f, p, where, row):
        start[f, p, where] = row

    def put_section(f, p, where, row):
        section[f, p, where] = row

    def put_beside(f, q, where, row):
        halo[q, f, 1 - q, where] = row

    def advance(get, p, r0, ahead_x, behind_x, border_ref):
        s = [get(f, p, padded(r0)) for f in range(5)]
        over_r = inv_r[r0 : r0 + SUB]
        over_rho = 1.0 / s[0]
        u, v, w = s[1], s[2], s[3]

        def grads(f):
            gx = ahead_x(f) - behind_x(f)
            gr = get(f, p, padded(r0, 1)) - get(f, p, padded(r0, -1))
            border = border_ref[f, p, r0 : r0 + SUB]
            ahead = jnp.where(sub_lane == local - 1, border, pltpu.roll(s[f], local - 1, 1))
            behind = jnp.where(sub_lane == 0, border, pltpu.roll(s[f], 1, 1))
            gt = (ahead - behind) * ((0.5 / angle_step) * over_r)
            return gx * (0.5 / spacing), gr * (0.5 / spacing), gt

        g = [grads(f) for f in range(5)]
        advect = [u * gx + v * gr + w * gt for gx, gr, gt in g]
        diverg = g[1][0] + g[2][1] + v * over_r + g[3][2]
        rates = (
            -advect[0] - s[0] * diverg,
            -advect[1] - g[4][0] * over_rho,
            -advect[2] + w * w * over_r - g[4][1] * over_rho,
            -advect[3] - v * w * over_r - g[4][2] * over_rho,
            -advect[4] - 1.4 * s[4] * diverg,
        )
        return s, [tau * rate for rate in rates]

    def advance_start(p, r0):
        here = padded(r0)
        if p == 0:
            ahead, behind = (lambda f: start[f, 1, here]), (lambda f: halo[0, f, 1, here])
        else:
            ahead, behind = (lambda f: halo[1, f, 0, here]), (lambda f: start[f, 0, here])
        return advance(own(start), p, r0, ahead, behind, edge)

    def advance_beside(q, r0):
        here = padded(r0)
        if q == 0:
            ahead, behind = (lambda f: start[f, 0, here]), (lambda f: halo[0, f, 0, here])
        else:
            ahead, behind = (lambda f: halo[1, f, 1, here]), (lambda f: start[f, 1, here])
        return advance(beside, q, r0, ahead, behind, edge_halo)

    def finish(p, r0):
        here, plain = padded(r0), slice(r0, r0 + SUB)
        if p == 0:
            ahead, behind = (lambda f: section[f, 1, here]), (lambda f: halo_next[0, f, plain])
        else:
            ahead, behind = (lambda f: halo_next[1, f, plain]), (lambda f: section[f, 0, here])
        s, step = advance(own(section), p, r0, ahead, behind, edge)
        for f in range(5):
            value = 0.5 * start[f, p, here] + 0.5 * (s[f] + step[f])
            target = dens_out if f == 0 else pres_out if f == 4 else velo_out.at[f - 1]
            target[p, plain] = value

    def pass_chunk(k):
        mate_copy(k).wait_recv()
        hop_copy(k).start()

    def take_chunk(k):
        hop_copy(k).wait_recv()
        send_edges(beside, 1, k)
        receive_edges(edge, 0, k)
        r0 = first_row(k)
        for p in range(2):
            s, step = advance_start(p, r0)
            for f in range(5):
                section[f, p, padded(r0)] = s[f] + step[f]
        send_edges(own(section), 2, k)

    def take_beside(k):
        receive_edges(edge_halo, 1, k)
        r0 = first_row(k)
        for q in range(2):
            s, step = advance_beside(q, r0)
            for f in range(5):
                halo_next[q, f, r0 : r0 + SUB] = s[f] + step[f]

    for load in loads[:3]:
        load.wait()
    for p in range(2):
        for f in range(5):
            gathered[0, 0, p, f * inner : (f + 1) * inner] = start[f, p, PAD : PAD + inner]
        send_inner(0, p)
    early = chunks // 2
    for k in range(early):
        mate_copy(k).start()
    wall(own(start), put_start)
    radius = (lax.broadcasted_iota(jnp.int32, (rows, local), 0).astype(jnp.float32) + 0.5) * spacing
    inv_r[...] = 1.0 / radius
    loads[3].wait()
    inverse[0:local] = forward[me]
    inverse[local : 2 * local] = jnp.zeros((local, inverse.shape[1]), jnp.float32)
    inverse[local : local + 1] = forward[left, local - 1 : local]
    inverse[2 * local - 1 : 2 * local] = forward[right, 0:1]
    inverse_high[...], inverse_low[...] = halves(inverse[...])
    for slot, owner in enumerate((me, mate, opposite, far)):
        span = slice(slot * local, (slot + 1) * local)
        basis_high[span], basis_low[span] = halves(forward[owner])
    modes = 2 * inner + 1
    column = lax.broadcasted_iota(jnp.int32, (1, weight.shape[1]), 1)
    mode = jnp.where(column < modes, column, column - (modes - 1))
    scale = jnp.where(column == 0, 1.0 / (4 * local), 2.0 / (4 * local))
    scale = jnp.where(column < 2 * modes - 1, scale, 0.0)
    for j in range(inner):
        weight[j : j + 1] = jnp.where(mode < cutoff[j], scale, 0.0)
    for p in range(2):
        pass_inner(0, p)
        pass_chunk(p)
    for k in range(chunks):
        send_edges(own(start), 0, k)
    filter_inner(start, 0)
    for k in range(early, chunks):
        mate_copy(k).start()

    for k in range(2, early):
        pass_chunk(k)
    for k in range(early):
        take_chunk(k)
    for copy in inner_copies(0):
        copy.wait_recv()
    for p in range(2):
        for r0 in range(0, inner, SUB):
            s, step = advance_start(p, r0)
            for f in range(5):
                gathered[1, 0, p, f * inner + r0 : f * inner + r0 + SUB] = s[f] + step[f]
        send_inner(1, p)
    for k in range(early - 1):
        take_beside(k)
    pass_chunk(early)
    for p in range(2):
        pass_inner(1, p)
        if early + 1 + p < chunks - 1:
            pass_chunk(early + 1 + p)
    filter_inner(section, 1)
    pass_chunk(chunks - 1)
    for k in range(early, chunks):
        take_chunk(k)
    wall(beside, put_beside)
    wall(own(section), put_section)
    for k in range(early - 1, chunks):
        take_beside(k)

    for k in range(chunks):
        receive_edges(edge, 2, k)
        for p in range(2):
            finish(p, first_row(k))
    for copy in inner_copies(1):
        copy.wait_recv()
    for p in range(2):
        for r0 in range(0, inner, SUB):
            finish(p, r0)

    for k in range(chunks):
        mate_copy(k).wait_send()
        hop_copy(k).wait_send()
        for kind in range(3):
            for copy in t_copies(kind, k):
                copy.wait_send()
    for stage in range(2):
        for copy in inner_copies(stage):
            copy.wait_send()
        for p in range(2):
            own_copy(stage, p, 0).wait_send()
            own_copy(stage, p, 1).wait_send()
            pass_copy(stage, p).wait_send()


def body(density, velocity, pressure, cutoff):
    planes, rows, local = density.shape
    points = local * lax.axis_size("sec")
    inner = rows // 4
    forward = tables(points, local, 2 * inner + 1)
    f32 = jnp.float32
    chunks = (rows - inner) // SUB
    vmem = pl.BlockSpec(memory_space=pltpu.VMEM)
    hbm = pl.BlockSpec(memory_space=pltpu.MemorySpace.HBM)
    run = pl.pallas_call(
        functools.partial(kernel, 1.0 / rows, 2.0 * math.pi / points, inner),
        out_shape=(
            jax.ShapeDtypeStruct(density.shape, f32),
            jax.ShapeDtypeStruct(velocity.shape, f32),
            jax.ShapeDtypeStruct(pressure.shape, f32),
        ),
        in_specs=[hbm] * 3 + [pl.BlockSpec(memory_space=pltpu.SMEM), hbm],
        out_specs=(vmem,) * 3,
        scratch_shapes=[
            pltpu.VMEM((5, planes, rows + 2 * PAD, local), f32),
            pltpu.VMEM((5, planes, rows + 2 * PAD, local), f32),
            pltpu.VMEM((2, 5, planes, rows + 2 * PAD, local), f32),
            pltpu.VMEM((2, 5, rows, local), f32),
            pltpu.VMEM((5, planes, rows, local), f32),
            pltpu.VMEM((5, 2, rows, local), f32),
            pltpu.VMEM((2, 4, planes, 5 * inner, local), f32),
            pltpu.VMEM((3, chunks, 8, local), f32),
            pltpu.VMEM((3, chunks, 8, local), f32),
            pltpu.VMEM((3, chunks, 8, local), f32),
            pltpu.VMEM((rows, local), f32),
            pltpu.VMEM((inner, forward.shape[2]), f32),
            pltpu.VMEM(forward.shape, f32),
            pltpu.VMEM((2 * local, forward.shape[2]), f32),
            pltpu.VMEM((points, forward.shape[2]), jnp.bfloat16),
            pltpu.VMEM((points, forward.shape[2]), jnp.bfloat16),
            pltpu.VMEM((2 * local, forward.shape[2]), jnp.bfloat16),
            pltpu.VMEM((2 * local, forward.shape[2]), jnp.bfloat16),
            pltpu.SemaphoreType.DMA((4,)),
            pltpu.SemaphoreType.DMA((2, planes, 3)),
            pltpu.SemaphoreType.DMA((2, planes, 3)),
            pltpu.SemaphoreType.DMA((2, 2)),
            pltpu.SemaphoreType.DMA((2, 2)),
            pltpu.SemaphoreType.DMA((chunks,)),
            pltpu.SemaphoreType.DMA((chunks,)),
            pltpu.SemaphoreType.DMA((chunks,)),
            pltpu.SemaphoreType.DMA((chunks,)),
            pltpu.SemaphoreType.DMA((3, chunks, 2)),
            pltpu.SemaphoreType.DMA((3, chunks, 2)),
        ],
        compiler_params=pltpu.CompilerParams(
            collective_id=0, has_side_effects=True, vmem_limit_bytes=62 * 1024 * 1024
        ),
    )
    return run(density, velocity, pressure, cutoff, jnp.asarray(forward))


def solution(mesh):
    return jax.shard_map(
        body,
        mesh=mesh,
        in_specs=(P("ax", None, "sec"), P(None, "ax", None, "sec"), P("ax", None, "sec"), P()),
        out_specs=(P("ax", None, "sec"), P(None, "ax", None, "sec"), P("ax", None, "sec")),
        check_vma=False,
    )
```

```python
import functools
import math

import jax
import jax.numpy as jnp
import numpy as np
from jax import lax
from jax.experimental import pallas as pl
from jax.experimental.pallas import tpu as pltpu
from jax.sharding import PartitionSpec as P

MESH = pl.DeviceIdType.MESH
PAD = 8
SUB = 32


def tables(points, local, modes):
    width = -(-(2 * modes - 1) // 128) * 128
    mode = np.zeros(width, np.int64)
    mode[:modes] = np.arange(modes)
    mode[modes : 2 * modes - 1] = np.arange(1, modes)

    def rows(index):
        angle = 2.0 * np.pi / points * ((index[:, None] * mode[None, :]) % points)
        out = np.where(np.arange(width) < modes, np.cos(angle), np.sin(angle))
        out[:, 2 * modes - 1 :] = 0.0
        return out

    sectors = points // local
    forward = rows(np.arange(points)).reshape(sectors, local, width)
    return forward.astype(np.float32)


def kernel(
    spacing, angle_step, inner,
    dens, velo, pres, cutoff, forward_in,
    dens_out, velo_out, pres_out,
    start, section, halo, halo_next, edge, edge_halo, gathered, pack, from_left, from_right, inv_r,
    weight, forward, inverse, basis_high, basis_low, inverse_high, inverse_low,
    load_sem, gather_send, gather_recv, x_send, x_recv, mate_send, mate_recv, hop_send, hop_recv,
    t_send, t_recv,
):
    rows, local = inv_r.shape
    chunks = (rows - inner) // SUB
    tau = 0.05 * spacing
    ax, n_ax = lax.axis_index("ax"), lax.axis_size("ax")
    me = lax.axis_index("sec")
    odd = lax.rem(ax, 2)
    before, after = lax.rem(ax + n_ax - 1, n_ax), lax.rem(ax + 1, n_ax)
    ax_mate = ax + 1 - 2 * odd
    hop_to = lax.rem(ax + 2 - 4 * odd + n_ax, n_ax)
    hop_from = lax.rem(ax - 2 + 4 * odd + n_ax, n_ax)
    left, right = lax.rem(me + 3, 4), lax.rem(me + 1, 4)
    mate = me + 1 - 2 * lax.rem(me, 2)
    opposite = lax.rem(me + 2, 4)
    far = lax.rem(mate + 2, 4)

    whole = pl.ds(PAD, rows)
    loads = [
        pltpu.make_async_copy(dens, start.at[0, :, whole], load_sem.at[0]),
        pltpu.make_async_copy(velo, start.at[1:4, :, whole], load_sem.at[1]),
        pltpu.make_async_copy(pres, start.at[4, :, whole], load_sem.at[2]),
        pltpu.make_async_copy(forward_in, forward, load_sem.at[3]),
    ]
    for load in loads:
        load.start()

    barrier = pltpu.get_barrier_semaphore()
    for target in (
        {"ax": before}, {"ax": after}, {"ax": hop_to}, {"ax": hop_from},
        {"sec": mate}, {"sec": opposite}, {"sec": far},
    ):
        pl.semaphore_signal(barrier, inc=1, device_id=target, device_id_type=MESH)
    pl.semaphore_wait(barrier, 7)

    def remote(src, dst, send, recv, target):
        return pltpu.make_async_remote_copy(
            src_ref=src, dst_ref=dst, send_sem=send, recv_sem=recv,
            device_id=target, device_id_type=MESH,
        )

    def inner_copies(stage):
        here = pl.ds(PAD, inner)
        if stage == 0:
            state, low, high = start, halo.at[0, :, 1, here], halo.at[1, :, 0, here]
        else:
            state, low, high = section, halo_next.at[0, :, 0:inner], halo_next.at[1, :, 0:inner]
        return (
            remote(state.at[:, 0, here], high, x_send.at[stage, 0], x_recv.at[stage, 0], {"ax": before}),
            remote(state.at[:, 1, here], low, x_send.at[stage, 1], x_recv.at[stage, 1], {"ax": after}),
        )

    def mate_copy(k):
        here = pl.ds(PAD + inner + k * SUB, SUB)
        return remote(start.at[:, :, here], halo.at[odd, :, :, here],
                      mate_send.at[k], mate_recv.at[k], {"ax": ax_mate})

    def hop_copy(k):
        here = pl.ds(PAD + inner + k * SUB, SUB)
        return remote(halo.at[1 - odd, :, :, here], halo.at[odd, :, :, here],
                      hop_send.at[k], hop_recv.at[k], {"ax": hop_to})

    def t_copies(kind, k):
        return (
            remote(pack.at[kind, k], from_right.at[kind, k],
                   t_send.at[kind, k, 0], t_recv.at[kind, k, 0], {"sec": left}),
            remote(pack.at[kind, k], from_left.at[kind, k],
                   t_send.at[kind, k, 1], t_recv.at[kind, k, 1], {"sec": right}),
        )

    def own_copy(stage, p, way):
        return remote(gathered.at[stage, 0, p], gathered.at[stage, 2 - way, p],
                      gather_send.at[stage, p, way], gather_recv.at[stage, p, way],
                      {"sec": mate if way else opposite})

    def pass_copy(stage, p):
        return remote(gathered.at[stage, 2, p], gathered.at[stage, 3, p],
                      gather_send.at[stage, p, 2], gather_recv.at[stage, p, 2], {"sec": mate})

    sub_lane = lax.broadcasted_iota(jnp.int32, (SUB, local), 1)

    def padded(r0, offset=0):
        return slice(PAD + r0 + offset, PAD + r0 + offset + SUB)

    def first_row(k):
        return inner + k * SUB

    def beside(f, q, where):
        return halo[q, f, 1 - q, where]

    def own(state):
        return lambda f, p, where: state[f, p, where]

    def send_edges(get, kind, k):
        packed = jnp.zeros((SUB, local), jnp.float32)
        for f in range(5):
            for p in range(2):
                i = 2 * f + p
                value = get(f, p, padded(first_row(k)))
                packed = jnp.where(sub_lane == i, pltpu.roll(value, (i + 1) % local, 1), packed)
                packed = jnp.where(sub_lane == 10 + i, pltpu.roll(value, 10 + i, 1), packed)
        folded = packed[0:8]
        for g in range(1, SUB // 8):
            folded = folded + pltpu.roll(packed[8 * g : 8 * g + 8], 32 * g, 1)
        pack[kind, k] = folded
        for copy in t_copies(kind, k):
            copy.start()

    def unfolded(value):
        parts = [value] + [pltpu.roll(value, local - 32 * g, 1) for g in range(1, SUB // 8)]
        return jnp.concatenate(parts, axis=0)

    def receive_edges(target, kind, k):
        for copy in t_copies(kind, k):
            copy.wait_recv()
        low, high = unfolded(from_left[kind, k]), unfolded(from_right[kind, k])
        r0 = first_row(k)
        for f in range(5):
            for p in range(2):
                i = 2 * f + p
                a = pltpu.roll(low, (local - i) % local, 1)
                b = pltpu.roll(high, local - 1 - (10 + i), 1)
                target[f, p, r0 : r0 + SUB] = jnp.where(sub_lane == 0, a, b)

    def send_inner(stage, p):
        own_copy(stage, p, 0).start()
        own_copy(stage, p, 1).start()

    def pass_inner(stage, p):
        own_copy(stage, p, 0).wait_recv()
        pass_copy(stage, p).start()

    def halves(value):
        high = value.astype(jnp.bfloat16)
        return high, (value - high.astype(jnp.float32)).astype(jnp.bfloat16)

    def product(value, basis_high, basis_low, dim):
        high, low = halves(value)

        def dot(a, b):
            return lax.dot_general(a, b, (((1,), (dim,)), ((), ())), preferred_element_type=jnp.float32)

        return dot(high, basis_high) + (dot(high, basis_low) + dot(low, basis_high))

    def filter_inner(state, stage):
        for p in range(2):
            own_copy(stage, p, 1).wait_recv()
            pass_copy(stage, p).wait_recv()
            values = jnp.concatenate([gathered[stage, slot, p] for slot in range(4)], axis=1)
            coeffs = product(values, basis_high[...], basis_low[...], 0)
            coeffs = coeffs.reshape(5, inner, -1) * weight[...][None]
            flat = coeffs.reshape(5 * inner, -1)
            both = product(flat, inverse_high[...], inverse_low[...], 1)
            across = product(coeffs[:, :8].reshape(40, -1), basis_high[2 * local : 3 * local],
                             basis_low[2 * local : 3 * local], 1)
            for f in range(5):
                state[f, p, PAD : PAD + inner] = both[f * inner : (f + 1) * inner, :local]
                edge[f, p, 0:inner] = both[f * inner : (f + 1) * inner, local:]
                row = across[8 * f : 8 * f + 1]
                state[f, p, PAD - 1 : PAD] = -row if f in (2, 3) else row
            inner_copies(stage)[p].start()

    def wall(get, put):
        for f in range(5):
            for p in range(2):
                row = get(f, p, slice(PAD + rows - 1, PAD + rows))
                put(f, p, slice(PAD + rows, PAD + rows + 1), -row if f == 2 else row)

    def put_start(f, p, where, row):
        start[f, p, where] = row

    def put_section(f, p, where, row):
        section[f, p, where] = row

    def put_beside(f, q, where, row):
        halo[q, f, 1 - q, where] = row

    def advance(get, p, r0, ahead_x, behind_x, border_ref):
        s = [get(f, p, padded(r0)) for f in range(5)]
        over_r = inv_r[r0 : r0 + SUB]
        over_rho = 1.0 / s[0]
        u, v, w = s[1], s[2], s[3]

        def grads(f):
            gx = ahead_x(f) - behind_x(f)
            gr = get(f, p, padded(r0, 1)) - get(f, p, padded(r0, -1))
            border = border_ref[f, p, r0 : r0 + SUB]
            ahead = jnp.where(sub_lane == local - 1, border, pltpu.roll(s[f], local - 1, 1))
            behind = jnp.where(sub_lane == 0, border, pltpu.roll(s[f], 1, 1))
            gt = (ahead - behind) * ((0.5 / angle_step) * over_r)
            return gx * (0.5 / spacing), gr * (0.5 / spacing), gt

        g = [grads(f) for f in range(5)]
        advect = [u * gx + v * gr + w * gt for gx, gr, gt in g]
        diverg = g[1][0] + g[2][1] + v * over_r + g[3][2]
        rates = (
            -advect[0] - s[0] * diverg,
            -advect[1] - g[4][0] * over_rho,
            -advect[2] + w * w * over_r - g[4][1] * over_rho,
            -advect[3] - v * w * over_r - g[4][2] * over_rho,
            -advect[4] - 1.4 * s[4] * diverg,
        )
        return s, [tau * rate for rate in rates]

    def advance_start(p, r0):
        here = padded(r0)
        if p == 0:
            ahead, behind = (lambda f: start[f, 1, here]), (lambda f: halo[0, f, 1, here])
        else:
            ahead, behind = (lambda f: halo[1, f, 0, here]), (lambda f: start[f, 0, here])
        return advance(own(start), p, r0, ahead, behind, edge)

    def advance_beside(q, r0):
        here = padded(r0)
        if q == 0:
            ahead, behind = (lambda f: start[f, 0, here]), (lambda f: halo[0, f, 0, here])
        else:
            ahead, behind = (lambda f: halo[1, f, 1, here]), (lambda f: start[f, 1, here])
        return advance(beside, q, r0, ahead, behind, edge_halo)

    def finish(p, r0):
        here, plain = padded(r0), slice(r0, r0 + SUB)
        if p == 0:
            ahead, behind = (lambda f: section[f, 1, here]), (lambda f: halo_next[0, f, plain])
        else:
            ahead, behind = (lambda f: halo_next[1, f, plain]), (lambda f: section[f, 0, here])
        s, step = advance(own(section), p, r0, ahead, behind, edge)
        for f in range(5):
            value = 0.5 * start[f, p, here] + 0.5 * (s[f] + step[f])
            target = dens_out if f == 0 else pres_out if f == 4 else velo_out.at[f - 1]
            target[p, plain] = value

    def pass_chunk(k):
        mate_copy(k).wait_recv()
        hop_copy(k).start()

    def take_chunk(k):
        hop_copy(k).wait_recv()
        send_edges(beside, 1, k)
        receive_edges(edge, 0, k)
        r0 = first_row(k)
        for p in range(2):
            s, step = advance_start(p, r0)
            for f in range(5):
                section[f, p, padded(r0)] = s[f] + step[f]
        send_edges(own(section), 2, k)

    def take_beside(k):
        receive_edges(edge_halo, 1, k)
        r0 = first_row(k)
        for q in range(2):
            s, step = advance_beside(q, r0)
            for f in range(5):
                halo_next[q, f, r0 : r0 + SUB] = s[f] + step[f]

    for load in loads[:3]:
        load.wait()
    for p in range(2):
        for f in range(5):
            gathered[0, 0, p, f * inner : (f + 1) * inner] = start[f, p, PAD : PAD + inner]
        send_inner(0, p)
    early = chunks // 2
    for k in range(early):
        mate_copy(k).start()
    for k in range(chunks):
        send_edges(own(start), 0, k)
    wall(own(start), put_start)
    radius = (lax.broadcasted_iota(jnp.int32, (rows, local), 0).astype(jnp.float32) + 0.5) * spacing
    inv_r[...] = 1.0 / radius
    loads[3].wait()
    inverse[0:local] = forward[me]
    inverse[local : 2 * local] = jnp.zeros((local, inverse.shape[1]), jnp.float32)
    inverse[local : local + 1] = forward[left, local - 1 : local]
    inverse[2 * local - 1 : 2 * local] = forward[right, 0:1]
    inverse_high[...], inverse_low[...] = halves(inverse[...])
    for slot, owner in enumerate((me, mate, opposite, far)):
        span = slice(slot * local, (slot + 1) * local)
        basis_high[span], basis_low[span] = halves(forward[owner])
    modes = 2 * inner + 1
    column = lax.broadcasted_iota(jnp.int32, (1, weight.shape[1]), 1)
    mode = jnp.where(column < modes, column, column - (modes - 1))
    scale = jnp.where(column == 0, 1.0 / (4 * local), 2.0 / (4 * local))
    scale = jnp.where(column < 2 * modes - 1, scale, 0.0)
    for j in range(inner):
        weight[j : j + 1] = jnp.where(mode < cutoff[j], scale, 0.0)
    for p in range(2):
        pass_inner(0, p)
        pass_chunk(p)
    filter_inner(start, 0)
    for k in range(early, chunks):
        mate_copy(k).start()

    for k in range(2, early):
        pass_chunk(k)
    for k in range(early):
        take_chunk(k)
    for copy in inner_copies(0):
        copy.wait_recv()
    for p in range(2):
        for r0 in range(0, inner, SUB):
            s, step = advance_start(p, r0)
            for f in range(5):
                gathered[1, 0, p, f * inner + r0 : f * inner + r0 + SUB] = s[f] + step[f]
        send_inner(1, p)
    for k in range(early - 1):
        take_beside(k)
    pass_chunk(early)
    for p in range(2):
        pass_inner(1, p)
        if early + 1 + p < chunks - 1:
            pass_chunk(early + 1 + p)
    filter_inner(section, 1)
    pass_chunk(chunks - 1)
    for k in range(early, chunks):
        take_chunk(k)
    wall(beside, put_beside)
    wall(own(section), put_section)
    for k in range(early - 1, chunks):
        take_beside(k)

    for k in range(chunks):
        receive_edges(edge, 2, k)
        for p in range(2):
            finish(p, first_row(k))
    for copy in inner_copies(1):
        copy.wait_recv()
    for p in range(2):
        for r0 in range(0, inner, SUB):
            finish(p, r0)

    for k in range(chunks):
        mate_copy(k).wait_send()
        hop_copy(k).wait_send()
        for kind in range(3):
            for copy in t_copies(kind, k):
                copy.wait_send()
    for stage in range(2):
        for copy in inner_copies(stage):
            copy.wait_send()
        for p in range(2):
            own_copy(stage, p, 0).wait_send()
            own_copy(stage, p, 1).wait_send()
            pass_copy(stage, p).wait_send()


def body(density, velocity, pressure, cutoff):
    planes, rows, local = density.shape
    points = local * lax.axis_size("sec")
    inner = rows // 4
    forward = tables(points, local, 2 * inner + 1)
    f32 = jnp.float32
    chunks = (rows - inner) // SUB
    vmem = pl.BlockSpec(memory_space=pltpu.VMEM)
    hbm = pl.BlockSpec(memory_space=pltpu.MemorySpace.HBM)
    run = pl.pallas_call(
        functools.partial(kernel, 1.0 / rows, 2.0 * math.pi / points, inner),
        out_shape=(
            jax.ShapeDtypeStruct(density.shape, f32),
            jax.ShapeDtypeStruct(velocity.shape, f32),
            jax.ShapeDtypeStruct(pressure.shape, f32),
        ),
        in_specs=[hbm] * 3 + [pl.BlockSpec(memory_space=pltpu.SMEM), hbm],
        out_specs=(vmem,) * 3,
        scratch_shapes=[
            pltpu.VMEM((5, planes, rows + 2 * PAD, local), f32),
            pltpu.VMEM((5, planes, rows + 2 * PAD, local), f32),
            pltpu.VMEM((2, 5, planes, rows + 2 * PAD, local), f32),
            pltpu.VMEM((2, 5, rows, local), f32),
            pltpu.VMEM((5, planes, rows, local), f32),
            pltpu.VMEM((5, 2, rows, local), f32),
            pltpu.VMEM((2, 4, planes, 5 * inner, local), f32),
            pltpu.VMEM((3, chunks, 8, local), f32),
            pltpu.VMEM((3, chunks, 8, local), f32),
            pltpu.VMEM((3, chunks, 8, local), f32),
            pltpu.VMEM((rows, local), f32),
            pltpu.VMEM((inner, forward.shape[2]), f32),
            pltpu.VMEM(forward.shape, f32),
            pltpu.VMEM((2 * local, forward.shape[2]), f32),
            pltpu.VMEM((points, forward.shape[2]), jnp.bfloat16),
            pltpu.VMEM((points, forward.shape[2]), jnp.bfloat16),
            pltpu.VMEM((2 * local, forward.shape[2]), jnp.bfloat16),
            pltpu.VMEM((2 * local, forward.shape[2]), jnp.bfloat16),
            pltpu.SemaphoreType.DMA((4,)),
            pltpu.SemaphoreType.DMA((2, planes, 3)),
            pltpu.SemaphoreType.DMA((2, planes, 3)),
            pltpu.SemaphoreType.DMA((2, 2)),
            pltpu.SemaphoreType.DMA((2, 2)),
            pltpu.SemaphoreType.DMA((chunks,)),
            pltpu.SemaphoreType.DMA((chunks,)),
            pltpu.SemaphoreType.DMA((chunks,)),
            pltpu.SemaphoreType.DMA((chunks,)),
            pltpu.SemaphoreType.DMA((3, chunks, 2)),
            pltpu.SemaphoreType.DMA((3, chunks, 2)),
        ],
        compiler_params=pltpu.CompilerParams(
            collective_id=0, has_side_effects=True, vmem_limit_bytes=62 * 1024 * 1024
        ),
    )
    return run(density, velocity, pressure, cutoff, jnp.asarray(forward))


def solution(mesh):
    return jax.shard_map(
        body,
        mesh=mesh,
        in_specs=(P("ax", None, "sec"), P(None, "ax", None, "sec"), P("ax", None, "sec"), P()),
        out_specs=(P("ax", None, "sec"), P(None, "ax", None, "sec"), P("ax", None, "sec")),
        check_vma=False,
    )
```
